32 devices in a mesh: tm: 8 (over y, x, core), space: 4 (over z).
Axes of the slice: x: 2, y: 2, z: 4, core: 2. Of those that a mesh axis runs over, the one named last changes fastest.
Arguments:
- increments: float32 [16, 256, 2048], P('tm', 'space'), may hold values from -6 to 6
- precision: float32 [16, 256, 2048], P('tm', 'space'), may hold values from 0.5 to 4
- courant_rows: float32 [256, 2048], P('space'), may hold values from 0.05 to 0.45
- courant_cols: float32 [256, 2048], P('space'), may hold values from 0.05 to 0.45
- wind_codes: int32 [16, 32, 16], P('tm', 'space'), may hold values from 0 to 3
Outputs:
- misfit: float32 [16, 256, 2048], P('tm', 'space')
- adjoint_image: float32 [16, 256, 2048], P('tm', 'space')
The draws below stay inside these ranges and needn't reach their ends.
All inputs are finite; a program needn't handle non-finite values.
Results may differ from the reference program's by a relative error of at most 0.00002.
Values sent between devices are 32-bit elements; how exact they have to be, the bound alone decides.
A program may use at most 64 MiB of HBM per device.

```python
import math
import jax
import jax.numpy as jnp

NY = 2048
BX = 8
BY = 128
SWEEPS = 2
STEPS = 16
NX = 256


def with_ends(array, rng, smallest, largest):
    longest = array.shape.index(max(array.shape))
    spots = []
    for shift in (0, 1):
        where = [jax.random.randint(jax.random.fold_in(rng, axis), (), 0, length) for axis, length in enumerate(array.shape)]
        where[longest] = (where[longest] + shift) % array.shape[longest]
        spots.append(tuple(where))
    return array.at[spots[0]].set(smallest).at[spots[1]].set(largest)


def levels(key, extent, cuts, low, high):
    factor_of = 1.0
    for axis_at, shards_of in cuts:
        draws = jax.random.uniform(jax.random.fold_in(jax.random.fold_in(key, 6), axis_at), (shards_of,), jnp.float32, low / len(cuts), high / len(cuts))
        factor_of = factor_of * jnp.repeat(jnp.exp(draws), extent[axis_at] // shards_of).reshape((-1,) + (1,) * (len(extent) - 1 - axis_at))
    return factor_of


def centred(key, extent, scale, most, cuts=(), dtype=jnp.bfloat16):
    drawn = scale * jax.random.normal(key, extent, jnp.float32)
    if cuts:
        drawn = drawn * levels(key, extent, cuts, -0.22, 0.18)
    return jnp.clip(drawn, -most, most).astype(dtype)


def setup_inputs(seed: int = 0) -> dict:
    key_of = jax.random.split(jax.random.key(seed), 6)
    return {
        "increments": centred(key_of[0], (STEPS, NX, NY), 1.0, 6.0, ((0, 8), (1, 4)), jnp.float32),
        "precision": jnp.clip(jnp.exp(math.log(4.0) - 2.0794415 * jax.random.uniform(key_of[1], (STEPS, NX, NY), jnp.float32) ** levels(key_of[1], (STEPS, NX, NY), ((0, 8), (1, 4)), -0.2, 0.2)), 0.5, 4.0),
        "courant_rows": jnp.clip(0.05 + 0.39999999 * jax.random.uniform(key_of[2], (NX, NY), jnp.float32) ** levels(key_of[2], (NX, NY), ((0, 4),), -0.2, 0.2), 0.05, 0.45),
        "courant_cols": jnp.clip(0.05 + 0.39999999 * jax.random.uniform(key_of[3], (NX, NY), jnp.float32) ** levels(key_of[3], (NX, NY), ((0, 4),), -0.2, 0.2), 0.05, 0.45),
        "wind_codes": with_ends(jax.random.randint(key_of[4], (STEPS, NX // BX, NY // BY), 0, 4), jax.random.fold_in(key_of[4], 1), 0, 3).astype(jnp.int32),
    }


def directions(wind_codes):
    per_cell = jnp.repeat(jnp.repeat(wind_codes, BX, axis=1), BY, axis=2)
    side_rows = 1 - 2 * (per_cell % 2)
    side_cols = 1 - 2 * (per_cell // 2)
    return side_rows, side_cols


def advance(values_in, padded, side_rows, side_cols, courant_rows, courant_cols):
    from_rows = jnp.where(side_rows > 0, padded[:, :-2], padded[:, 2:])
    from_cols = jnp.where(side_cols > 0, jnp.roll(values_in, 1, axis=2), jnp.roll(values_in, -1, axis=2))
    return (1.0 - courant_rows - courant_cols) * values_in + courant_rows * from_rows + courant_cols * from_cols


def smooth(values_in):
    field = values_in
    for sweep in range(SWEEPS):
        padded = jnp.pad(field, ((0, 0), (1, 1), (0, 0)))
        beside_all = padded[:, :-2] + padded[:, 2:] + jnp.roll(field, 1, axis=2) + jnp.roll(field, -1, axis=2)
        field = field + 0.2 * (beside_all - 4.0 * field)
    return field


def adjoint_pieces(values_in, side_rows, courant_rows):
    along_rows = courant_rows * values_in
    return jnp.stack([jnp.where(side_rows > 0, along_rows, 0.0), jnp.where(side_rows < 0, along_rows, 0.0)], axis=1)


def retreat(values_in, padded_pieces, side_rows, side_cols, courant_rows, courant_cols):
    from_rows = padded_pieces[:, 0, 2:] + padded_pieces[:, 1, :-2]
    along_cols = courant_cols * values_in
    plus_cols = jnp.where(side_cols > 0, along_cols, 0.0)
    minus_cols = jnp.where(side_cols < 0, along_cols, 0.0)
    from_cols = jnp.roll(plus_cols, -1, axis=2) + jnp.roll(minus_cols, 1, axis=2)
    return (1.0 - courant_rows - courant_cols) * values_in + from_rows + from_cols


def reference(increments, precision, courant_rows, courant_cols, wind_codes):
    side_rows, side_cols = directions(wind_codes)
    shifted = jnp.concatenate([jnp.zeros_like(increments[:1]), increments[:-1]], axis=0)
    padded = jnp.pad(shifted, ((0, 0), (1, 1), (0, 0)))
    moved = advance(shifted, padded, side_rows, side_cols, courant_rows, courant_cols)
    misfit = increments - moved
    weighted = smooth(precision * smooth(misfit))
    pieces = adjoint_pieces(weighted, side_rows, courant_rows)
    padded_pieces = jnp.pad(pieces, ((0, 0), (0, 0), (1, 1), (0, 0)))
    images = retreat(weighted, padded_pieces, side_rows, side_cols, courant_rows, courant_cols)
    following = jnp.concatenate([images[1:], jnp.zeros_like(images[:1])], axis=0)
    adjoint_image = weighted - following
    return misfit, adjoint_image
```

```python
import functools

import jax
import jax.numpy as jnp
from jax import lax
from jax.experimental import pallas as pl
from jax.experimental.pallas import tpu as pltpu
from jax.sharding import PartitionSpec as P

BX = 8
BY = 128
SWEEPS = 2
CHUNKS = 4
MESH = pl.DeviceIdType.MESH


def kernel(
    inc, prec, crow, ccol, codes,
    misfit_out, adjoint_out,
    incx, precx, cx, codex, cexp, ms, fa, fb, w, dn, up_, img, back, adj,
    local_sem, out_sem, zsend, zrecv, tsend, trecv, bsend, brecv,
):
    rows, cols = crow.shape
    blocks = rows // BX
    ext = rows + 2 * BX
    s = lax.axis_index("space")
    t = lax.axis_index("tm")
    n_s = lax.axis_size("space")
    n_t = lax.axis_size("tm")
    has_lo, has_hi = s > 0, s < n_s - 1
    has_prev, has_next = t > 0, t < n_t - 1
    own = pl.ds(BX, rows)
    top = pl.ds(0, BX)
    bottom = pl.ds(BX + rows, BX)
    first = pl.ds(0, BX)
    last = pl.ds(rows - BX, BX)
    chunk = rows // CHUNKS

    neighbours = (
        (has_lo, {"space": s - 1}),
        (has_hi, {"space": s + 1}),
        (has_prev, {"tm": t - 1}),
        (has_next, {"tm": t + 1}),
    )

    loads = [
        pltpu.make_async_copy(inc, incx.at[pl.ds(1, 2), own], local_sem.at[0]),
        pltpu.make_async_copy(crow, cx.at[0, own], local_sem.at[1]),
        pltpu.make_async_copy(ccol, cx.at[1, own], local_sem.at[2]),
        pltpu.make_async_copy(codes, codex.at[1], local_sem.at[3]),
        pltpu.make_async_copy(prec, precx.at[:, own], local_sem.at[4]),
    ]
    for load in loads:
        load.start()

    barrier = pltpu.get_barrier_semaphore()
    for there, where in neighbours:
        @pl.when(there)
        def _(where=where):
            pl.semaphore_signal(barrier, inc=1, device_id=where, device_id_type=MESH)
    count = sum(there.astype(jnp.int32) for there, _ in neighbours)
    pl.semaphore_wait(barrier, count)

    def remote(src, dst, send, recv, where):
        return pltpu.make_async_remote_copy(
            src_ref=src, dst_ref=dst, send_sem=send, recv_sem=recv,
            device_id=where, device_id_type=MESH,
        )

    def z_copies(side):
        edge = first if side == 0 else last
        halo = bottom if side == 0 else top
        where = {"space": s - 1} if side == 0 else {"space": s + 1}
        pairs = [
            (inc.at[:, edge], incx.at[pl.ds(1, 2), halo]),
            (crow.at[edge], cx.at[0, halo]),
            (ccol.at[edge], cx.at[1, halo]),
            (codes, codex.at[2 if side == 0 else 0]),
            (prec.at[:, edge], precx.at[:, halo]),
        ]
        return [
            remote(src, dst, zsend.at[side, i], zrecv.at[side, i], where)
            for i, (src, dst) in enumerate(pairs)
        ]

    forward = remote(inc.at[1], incx.at[0, own], tsend.at[0], trecv.at[0], {"tm": t + 1})
    relay_top = remote(incx.at[2, top], incx.at[0, top], tsend.at[1], trecv.at[1], {"tm": t + 1})
    relay_bottom = remote(incx.at[2, bottom], incx.at[0, bottom], tsend.at[2], trecv.at[2], {"tm": t + 1})

    def back_copy(i):
        part = pl.ds(i * chunk, chunk)
        return remote(img.at[0, part], back.at[part], bsend.at[i], brecv.at[i], {"tm": t - 1})

    @pl.when(has_next)
    def _():
        forward.start()

    sent_to = ((0, has_lo), (1, has_hi))
    arrives = ((0, has_hi), (1, has_lo))
    to_side = {0: z_copies(0), 1: z_copies(1)}
    for i in range(5):
        for side, there in sent_to:
            @pl.when(there)
            def _(side=side, i=i):
                to_side[side][i].start()

    def clear(ref_rows):
        for k in range(3):
            incx[k, ref_rows, :] = jnp.zeros((BX, cols), jnp.float32)
        for k in range(2):
            precx[k, ref_rows, :] = jnp.zeros((BX, cols), jnp.float32)
            cx[k, ref_rows, :] = jnp.zeros((BX, cols), jnp.float32)

    @pl.when(jnp.logical_not(has_lo))
    def _():
        clear(top)
        codex[0] = jnp.zeros(codex.shape[1:], jnp.int32)

    @pl.when(jnp.logical_not(has_hi))
    def _():
        clear(bottom)
        codex[2] = jnp.zeros(codex.shape[1:], jnp.int32)

    @pl.when(jnp.logical_not(has_prev))
    def _():
        incx[0] = jnp.zeros((ext, cols), jnp.float32)

    @pl.when(jnp.logical_not(has_next))
    def _():
        back[...] = jnp.zeros((rows, cols), jnp.float32)

    def arrived(i):
        for side, there in arrives:
            @pl.when(there)
            def _(side=side):
                to_side[side][i].wait_recv()

    loads[0].wait()
    arrived(0)

    @pl.when(has_next & has_lo)
    def _():
        relay_top.start()

    @pl.when(has_next & has_hi)
    def _():
        relay_bottom.start()

    for i in (1, 2, 3):
        loads[i].wait()
        arrived(i)

    for part in range(3):
        for k in range(2):
            value = codex[part, k]
            for j in range(cols // BY):
                cexp[k, pl.ds(part * blocks, blocks), pl.ds(j * BY, BY)] = jnp.broadcast_to(
                    value[:, j : j + 1], (blocks, BY)
                )

    row = lax.broadcasted_iota(jnp.int32, (BX, cols), 0)
    is_first, is_last = row == 0, row == BX - 1

    def at(b):
        return pl.ds(pl.multiple_of(b * BX, BX), BX)

    def above(ref, k, b, cur):
        prev = ref[k, at(jnp.maximum(b - 1, 0)), :]
        return pltpu.roll(jnp.where(is_last, prev, cur), 1, 0)

    def below(ref, k, b, cur):
        after = ref[k, at(jnp.minimum(b + 1, blocks + 1)), :]
        return pltpu.roll(jnp.where(is_first, after, cur), BX - 1, 0)

    def left(cur):
        return pltpu.roll(cur, 1, 1)

    def right(cur):
        return pltpu.roll(cur, cols - 1, 1)

    def inside(b, value):
        keep = ((b > 0) | has_lo) & ((b < blocks + 1) | has_hi)
        return jnp.where(keep, value, 0.0)

    def code_of(k, b):
        return jnp.broadcast_to(cexp[k, pl.ds(b + blocks - 1, 1), :], (BX, cols))

    def star(ref, k, b):
        cur = ref[k, at(b), :]
        return cur + above(ref, k, b, cur) + below(ref, k, b, cur) + (left(cur) + right(cur))

    def misfits(k):
        def body(b, carry):
            cur = incx[k, at(b), :]
            code = code_of(k, b)
            from_rows = jnp.where(code % 2 == 0, above(incx, k, b, cur), below(incx, k, b, cur))
            from_cols = jnp.where(code < 2, left(cur), right(cur))
            moved = cur + cx[0, at(b), :] * (from_rows - cur) + cx[1, at(b), :] * (from_cols - cur)
            ms[k, at(b), :] = inside(b, incx[k + 1, at(b), :] - moved)
            return carry

        lax.fori_loop(0, blocks + 2, body, 0)

    def sweep(src, dst, k, scale=None):
        def body(b, carry):
            value = star(src, k, b)
            if scale is not None:
                value = scale[k, at(b), :] * value
            dst[k, at(b), :] = inside(b, value)
            return carry

        lax.fori_loop(0, blocks + 2, body, 0)

    def weigh(k):
        def body(b, carry):
            value = inside(b, star(fa, k, b) * (0.2 ** (2 * SWEEPS)))
            code = code_of(k, b)
            along = cx[0, at(b), :] * value
            w[k, at(b), :] = value
            dn[k, at(b), :] = jnp.where(code % 2 == 0, along, 0.0)
            up_[k, at(b), :] = jnp.where(code % 2 == 0, 0.0, along)
            return carry

        lax.fori_loop(0, blocks + 2, body, 0)

    def retreat(k, start, stop):
        def body(b, carry):
            value = w[k, at(b), :]
            code = code_of(k, b)
            d, u = dn[k, at(b), :], up_[k, at(b), :]
            cols_part = cx[1, at(b), :] * value
            plus = jnp.where(code < 2, cols_part, 0.0)
            minus = cols_part - plus
            image = (
                value - (d + u) - cols_part
                + below(dn, k, b, d) + above(up_, k, b, u)
                + right(plus) + left(minus)
            )
            img[k, at(b - 1), :] = image
            if k == 0:
                adj[0, at(b - 1), :] = value - img[1, at(b - 1), :]
            return carry

        lax.fori_loop(start, stop, body, 0)

    misfit_copies = [
        pltpu.make_async_copy(ms.at[k, own], misfit_out.at[k], out_sem.at[k]) for k in range(2)
    ]

    def half_one(k):
        misfits(k)
        misfit_copies[k].start()
        sweep(ms, fa, k)

    def half_two(k):
        sweep(fa, fb, k, precx)
        sweep(fb, fa, k)
        weigh(k)

    half_one(1)
    loads[4].wait()
    arrived(4)
    half_two(1)
    retreat(1, 1, blocks + 1)

    @pl.when(has_prev)
    def _():
        forward.wait_recv()

    @pl.when(has_prev & has_lo)
    def _():
        relay_top.wait_recv()

    @pl.when(has_prev & has_hi)
    def _():
        relay_bottom.wait_recv()

    half_one(0)
    half_two(0)
    per_chunk = chunk // BX
    for i in range(CHUNKS):
        retreat(0, 1 + i * per_chunk, 1 + (i + 1) * per_chunk)

        @pl.when(has_prev)
        def _(i=i):
            back_copy(i).start()

    out0 = pltpu.make_async_copy(adj.at[0], adjoint_out.at[0], out_sem.at[2])
    out0.start()

    for i in range(CHUNKS):
        @pl.when(has_next)
        def _(i=i):
            back_copy(i).wait_recv()

        def body(b, carry):
            adj[1, at(b), :] = w[1, at(b + 1), :] - back[at(b), :]
            return carry

        lax.fori_loop(i * per_chunk, (i + 1) * per_chunk, body, 0)
    out1 = pltpu.make_async_copy(adj.at[1], adjoint_out.at[1], out_sem.at[3])
    out1.start()

    for side, there in sent_to:
        @pl.when(there)
        def _(side=side):
            for copy in to_side[side]:
                copy.wait_send()

    @pl.when(has_next)
    def _():
        forward.wait_send()

    @pl.when(has_next & has_lo)
    def _():
        relay_top.wait_send()

    @pl.when(has_next & has_hi)
    def _():
        relay_bottom.wait_send()

    @pl.when(has_prev)
    def _():
        for i in range(CHUNKS):
            back_copy(i).wait_send()

    for copy in misfit_copies:
        copy.wait()
    out0.wait()
    out1.wait()


def on_device(increments, precision, courant_rows, courant_cols, wind_codes):
    steps, rows, cols = increments.shape
    ext = rows + 2 * BX
    f32 = jnp.float32
    anywhere = pl.BlockSpec(memory_space=pl.ANY)
    out = jax.ShapeDtypeStruct(increments.shape, f32)
    field = pltpu.VMEM((2, ext, cols), f32)
    dma = pltpu.SemaphoreType.DMA
    return pl.pallas_call(
        kernel,
        name="window",
        out_shape=(out, out),
        in_specs=[anywhere] * 5,
        out_specs=(anywhere, anywhere),
        scratch_shapes=[
            pltpu.VMEM((3, ext, cols), f32),
            field,
            field,
            pltpu.VMEM((3,) + wind_codes.shape, jnp.int32),
            pltpu.VMEM((2, 3 * (rows // BX), cols), jnp.int32),
            field,
            field,
            field,
            field,
            field,
            field,
            pltpu.VMEM((2, rows, cols), f32),
            pltpu.VMEM((rows, cols), f32),
            pltpu.VMEM((2, rows, cols), f32),
            dma((5,)),
            dma((4,)),
            dma((2, 5)),
            dma((2, 5)),
            dma((3,)),
            dma((3,)),
            dma((CHUNKS,)),
            dma((CHUNKS,)),
        ],
        compiler_params=pltpu.CompilerParams(
            collective_id=0, has_side_effects=True, vmem_limit_bytes=40 << 20
        ),
    )(increments, precision, courant_rows, courant_cols, wind_codes)


def solution(mesh):
    in_specs = (
        P("tm", "space", None),
        P("tm", "space", None),
        P("space", None),
        P("space", None),
        P("tm", "space", None),
    )
    out_specs = (P("tm", "space", None), P("tm", "space", None))
    return jax.shard_map(
        on_device, mesh=mesh, in_specs=in_specs, out_specs=out_specs, check_vma=False
    )
```

```python
import functools

import jax
import jax.numpy as jnp
from jax import lax
from jax.experimental import pallas as pl
from jax.experimental.pallas import tpu as pltpu
from jax.sharding import PartitionSpec as P

BX = 8
BY = 128
SWEEPS = 2
MESH = pl.DeviceIdType.MESH


def chunks_of(blocks):
    middle = [(b, min(2, blocks - b)) for b in range(2, blocks, 2)]
    return middle + [(1, 1), (blocks, 1)]


def kernel(
    inc, prec, crow, ccol, codes,
    misfit_out, adjoint_out,
    incx, precx, cx, codex, cexp, ms, f1, f2, f3, w, dn, up_, img, back, adj,
    local_sem, out_sem, zsend, zrecv, tsend, trecv, bsend, brecv,
):
    rows, cols = crow.shape
    blocks = rows // BX
    ext = rows + 2 * BX
    s = lax.axis_index("space")
    t = lax.axis_index("tm")
    n_s = lax.axis_size("space")
    n_t = lax.axis_size("tm")
    has_lo, has_hi = s > 0, s < n_s - 1
    has_prev, has_next = t > 0, t < n_t - 1
    own = pl.ds(BX, rows)
    top = pl.ds(0, BX)
    bottom = pl.ds(BX + rows, BX)
    first = pl.ds(0, BX)
    last = pl.ds(rows - BX, BX)
    parts = chunks_of(blocks)

    neighbours = (
        (has_lo, {"space": s - 1}),
        (has_hi, {"space": s + 1}),
        (has_prev, {"tm": t - 1}),
        (has_next, {"tm": t + 1}),
    )

    loads = [
        pltpu.make_async_copy(inc, incx.at[pl.ds(1, 2), own], local_sem.at[0]),
        pltpu.make_async_copy(crow, cx.at[0, own], local_sem.at[1]),
        pltpu.make_async_copy(ccol, cx.at[1, own], local_sem.at[2]),
        pltpu.make_async_copy(codes, codex.at[1], local_sem.at[3]),
        pltpu.make_async_copy(prec, precx.at[:, own], local_sem.at[4]),
    ]
    for load in loads:
        load.start()

    barrier = pltpu.get_barrier_semaphore()
    for there, where in neighbours:
        @pl.when(there)
        def _(where=where):
            pl.semaphore_signal(barrier, inc=1, device_id=where, device_id_type=MESH)
    count = sum(there.astype(jnp.int32) for there, _ in neighbours)
    pl.semaphore_wait(barrier, count)

    def remote(src, dst, send, recv, where):
        return pltpu.make_async_remote_copy(
            src_ref=src, dst_ref=dst, send_sem=send, recv_sem=recv,
            device_id=where, device_id_type=MESH,
        )

    def z_copies(side):
        edge = first if side == 0 else last
        halo = bottom if side == 0 else top
        where = {"space": s - 1} if side == 0 else {"space": s + 1}
        pairs = [
            (inc.at[:, edge], incx.at[pl.ds(1, 2), halo]),
            (crow.at[edge], cx.at[0, halo]),
            (ccol.at[edge], cx.at[1, halo]),
            (codes, codex.at[2 if side == 0 else 0]),
            (prec.at[:, edge], precx.at[:, halo]),
        ]
        return [
            remote(src, dst, zsend.at[side, i], zrecv.at[side, i], where)
            for i, (src, dst) in enumerate(pairs)
        ]

    forward = remote(inc.at[1], incx.at[0, own], tsend.at[0], trecv.at[0], {"tm": t + 1})
    relay_top = remote(incx.at[2, top], incx.at[0, top], tsend.at[1], trecv.at[1], {"tm": t + 1})
    relay_bottom = remote(incx.at[2, bottom], incx.at[0, bottom], tsend.at[2], trecv.at[2], {"tm": t + 1})

    def back_copy(i):
        part = pl.ds((parts[i][0] - 1) * BX, parts[i][1] * BX)
        return remote(img.at[part], back.at[part], bsend.at[i], brecv.at[i], {"tm": t - 1})

    @pl.when(has_next)
    def _():
        forward.start()

    sent_to = ((0, has_lo), (1, has_hi))
    arrives = ((0, has_hi), (1, has_lo))
    to_side = {0: z_copies(0), 1: z_copies(1)}
    for i in range(5):
        for side, there in sent_to:
            @pl.when(there)
            def _(side=side, i=i):
                to_side[side][i].start()

    def clear(ref_rows):
        for k in range(3):
            incx[k, ref_rows, :] = jnp.zeros((BX, cols), jnp.float32)
        for k in range(2):
            precx[k, ref_rows, :] = jnp.zeros((BX, cols), jnp.float32)
            cx[k, ref_rows, :] = jnp.zeros((BX, cols), jnp.float32)

    @pl.when(jnp.logical_not(has_lo))
    def _():
        clear(top)
        codex[0] = jnp.zeros(codex.shape[1:], jnp.int32)

    @pl.when(jnp.logical_not(has_hi))
    def _():
        clear(bottom)
        codex[2] = jnp.zeros(codex.shape[1:], jnp.int32)

    @pl.when(jnp.logical_not(has_prev))
    def _():
        incx[0] = jnp.zeros((ext, cols), jnp.float32)

    @pl.when(jnp.logical_not(has_next))
    def _():
        back[...] = jnp.zeros((rows, cols), jnp.float32)

    def arrived(i):
        for side, there in arrives:
            @pl.when(there)
            def _(side=side):
                to_side[side][i].wait_recv()

    def expand(part):
        for k in range(2):
            value = codex[part, k]
            for j in range(cols // BY):
                cexp[k, pl.ds(part * blocks, blocks), pl.ds(j * BY, BY)] = jnp.broadcast_to(
                    value[:, j : j + 1], (blocks, BY)
                )

    row = lax.broadcasted_iota(jnp.int32, (BX, cols), 0)
    is_first, is_last = row == 0, row == BX - 1

    def at(b):
        return pl.ds(pl.multiple_of(b * BX, BX), BX)

    def left(cur):
        return pltpu.roll(cur, 1, 1)

    def right(cur):
        return pltpu.roll(cur, cols - 1, 1)

    def code_of(k, b):
        return jnp.broadcast_to(cexp[k, pl.ds(b + blocks - 1, 1), :], (BX, cols))

    def stages(k, edges):
        low, high = (0, blocks + 1) if edges else (1, blocks)

        def each(body):
            def step(i, carry):
                body(i + jnp.where(i >= 2, blocks - 2, 0) if edges else i + 1)
                return carry

            trips = 4 if edges else blocks
            lax.fori_loop(0, trips, step, 0, unroll=trips)

        def above(ref, b, cur):
            prev = ref[k, at(jnp.maximum(b - 1, low)), :]
            return pltpu.roll(jnp.where(is_last, prev, cur), 1, 0)

        def below(ref, b, cur):
            after = ref[k, at(jnp.minimum(b + 1, high)), :]
            return pltpu.roll(jnp.where(is_first, after, cur), BX - 1, 0)

        def inside(b, value):
            if not edges:
                return value
            keep = ((b > 0) | has_lo) & ((b < blocks + 1) | has_hi)
            return jnp.where(keep, value, 0.0)

        def star(ref, b):
            cur = ref[k, at(b), :]
            return cur + above(ref, b, cur) + below(ref, b, cur) + (left(cur) + right(cur))

        def misfit(b):
            cur = incx[k, at(b), :]
            code = code_of(k, b)
            from_rows = jnp.where((code & 1) == 0, above(incx, b, cur), below(incx, b, cur))
            from_cols = jnp.where(code < 2, left(cur), right(cur))
            moved = cur + cx[0, at(b), :] * (from_rows - cur) + cx[1, at(b), :] * (from_cols - cur)
            ms[k, at(b), :] = inside(b, incx[k + 1, at(b), :] - moved)

        def first_sweep(b):
            f1[k, at(b), :] = inside(b, star(ms, b))

        def second_sweep(b):
            f2[k, at(b), :] = inside(b, precx[k, at(b), :] * star(f1, b))

        def third_sweep(b):
            f3[k, at(b), :] = inside(b, star(f2, b))

        def weigh(b):
            value = inside(b, star(f3, b) * (0.2 ** (2 * SWEEPS)))
            lower = (code_of(k, b) & 1) == 0
            along = cx[0, at(b), :] * value
            w[k, at(b), :] = value
            dn[k, at(b), :] = jnp.where(lower, along, 0.0)
            up_[k, at(b), :] = jnp.where(lower, 0.0, along)

        for body in (misfit, first_sweep, second_sweep, third_sweep, weigh):
            each(body)

    def retreat(k, start, size):
        def body(i, carry):
            b = i + start
            value = w[k, at(b), :]
            d, u = dn[k, at(b), :], up_[k, at(b), :]
            after, prev = dn[k, at(b + 1), :], up_[k, at(b - 1), :]
            along = cx[1, at(b), :] * value
            plus = jnp.where(code_of(k, b) < 2, along, 0.0)
            image = (
                value - (d + u) - along
                + pltpu.roll(jnp.where(is_first, after, d), BX - 1, 0)
                + pltpu.roll(jnp.where(is_last, prev, u), 1, 0)
                + right(plus) + left(along - plus)
            )
            if k == 0:
                img[at(b - 1), :] = image
            else:
                adj[0, at(b - 1), :] = w[0, at(b), :] - image
            return carry

        lax.fori_loop(0, size, body, 0, unroll=size)

    def send_back(i):
        retreat(0, *parts[i])

        @pl.when(has_prev)
        def _():
            back_copy(i).start()

    for i in (0, 1, 2, 3):
        loads[i].wait()
    expand(1)
    loads[4].wait()
    stages(1, False)

    arrived(0)

    @pl.when(has_next & has_lo)
    def _():
        relay_top.start()

    @pl.when(has_next & has_hi)
    def _():
        relay_bottom.start()

    @pl.when(has_prev)
    def _():
        forward.wait_recv()

    stages(0, False)
    for i in range(len(parts) - 2):
        send_back(i)

    for i in (1, 2, 3, 4):
        arrived(i)
    expand(0)
    expand(2)

    @pl.when(has_prev & has_lo)
    def _():
        relay_top.wait_recv()

    @pl.when(has_prev & has_hi)
    def _():
        relay_bottom.wait_recv()

    stages(0, True)
    for i in (len(parts) - 2, len(parts) - 1):
        send_back(i)
    stages(1, True)
    misfit_copies = [
        pltpu.make_async_copy(ms.at[k, own], misfit_out.at[k], out_sem.at[k]) for k in range(2)
    ]
    for copy in misfit_copies:
        copy.start()
    retreat(1, 1, blocks)
    out0 = pltpu.make_async_copy(adj.at[0], adjoint_out.at[0], out_sem.at[2])
    out0.start()

    for i, (start, size) in enumerate(parts):
        @pl.when(has_next)
        def _(i=i):
            back_copy(i).wait_recv()

        for b in range(start, start + size):
            adj[1, at(b - 1), :] = w[1, at(b), :] - back[at(b - 1), :]
    out1 = pltpu.make_async_copy(adj.at[1], adjoint_out.at[1], out_sem.at[3])
    out1.start()

    for side, there in sent_to:
        @pl.when(there)
        def _(side=side):
            for copy in to_side[side]:
                copy.wait_send()

    @pl.when(has_next)
    def _():
        forward.wait_send()

    @pl.when(has_next & has_lo)
    def _():
        relay_top.wait_send()

    @pl.when(has_next & has_hi)
    def _():
        relay_bottom.wait_send()

    @pl.when(has_prev)
    def _():
        for i in range(len(parts)):
            back_copy(i).wait_send()

    for copy in misfit_copies:
        copy.wait()
    out0.wait()
    out1.wait()


def on_device(increments, precision, courant_rows, courant_cols, wind_codes):
    steps, rows, cols = increments.shape
    ext = rows + 2 * BX
    f32 = jnp.float32
    anywhere = pl.BlockSpec(memory_space=pl.ANY)
    in_hbm = pl.BlockSpec(memory_space=pltpu.MemorySpace.HBM)
    out = jax.ShapeDtypeStruct(increments.shape, f32)
    field = pltpu.VMEM((2, ext, cols), f32)
    dma = pltpu.SemaphoreType.DMA
    return pl.pallas_call(
        kernel,
        name="window",
        out_shape=(out, out),
        in_specs=[in_hbm] * 5,
        out_specs=(anywhere, anywhere),
        scratch_shapes=[
            pltpu.VMEM((3, ext, cols), f32),
            field,
            field,
            pltpu.VMEM((3,) + wind_codes.shape, jnp.int32),
            pltpu.VMEM((2, 3 * (rows // BX), cols), jnp.int32),
            field,
            field,
            field,
            field,
            field,
            field,
            field,
            pltpu.VMEM((rows, cols), f32),
            pltpu.VMEM((rows, cols), f32),
            pltpu.VMEM((2, rows, cols), f32),
            dma((5,)),
            dma((4,)),
            dma((2, 5)),
            dma((2, 5)),
            dma((3,)),
            dma((3,)),
            dma((len(chunks_of(rows // BX)),)),
            dma((len(chunks_of(rows // BX)),)),
        ],
        compiler_params=pltpu.CompilerParams(
            collective_id=0, has_side_effects=True, vmem_limit_bytes=60 << 20
        ),
    )(increments, precision, courant_rows, courant_cols, wind_codes)


def solution(mesh):
    in_specs = (
        P("tm", "space", None),
        P("tm", "space", None),
        P("space", None),
        P("space", None),
        P("tm", "space", None),
    )
    out_specs = (P("tm", "space", None), P("tm", "space", None))
    return jax.shard_map(
        on_device, mesh=mesh, in_specs=in_specs, out_specs=out_specs, check_vma=False
    )
```

```python
import functools

import jax
import jax.numpy as jnp
from jax import lax
from jax.experimental import pallas as pl
from jax.experimental.pallas import tpu as pltpu
from jax.sharding import PartitionSpec as P

BX = 8
BY = 128
SWEEPS = 2
MESH = pl.DeviceIdType.MESH


def chunks_of(blocks):
    middle = [(b, min(2, blocks - b)) for b in range(2, blocks, 2)]
    return middle + [(1, 1), (blocks, 1)]


def kernel(
    inc, prec, crow, ccol, codes,
    misfit_out, adj,
    incx, precx, cx, codex, cexp, ms, f1, f2, f3, w, dn, up_, img, back,
    local_sem, out_sem, zsend, zrecv, tsend, trecv, bsend, brecv,
):
    rows, cols = crow.shape
    blocks = rows // BX
    ext = rows + 2 * BX
    s = lax.axis_index("space")
    t = lax.axis_index("tm")
    n_s = lax.axis_size("space")
    n_t = lax.axis_size("tm")
    has_lo, has_hi = s > 0, s < n_s - 1
    has_prev, has_next = t > 0, t < n_t - 1
    own = pl.ds(BX, rows)
    top = pl.ds(0, BX)
    bottom = pl.ds(BX + rows, BX)
    first = pl.ds(0, BX)
    last = pl.ds(rows - BX, BX)
    parts = chunks_of(blocks)

    neighbours = (
        (has_lo, {"space": s - 1}),
        (has_hi, {"space": s + 1}),
        (has_prev, {"tm": t - 1}),
        (has_next, {"tm": t + 1}),
    )

    loads = [
        pltpu.make_async_copy(inc, incx.at[pl.ds(1, 2), own], local_sem.at[0]),
        pltpu.make_async_copy(crow, cx.at[0, own], local_sem.at[1]),
        pltpu.make_async_copy(ccol, cx.at[1, own], local_sem.at[2]),
        pltpu.make_async_copy(codes, codex.at[1], local_sem.at[3]),
        pltpu.make_async_copy(prec, precx.at[:, own], local_sem.at[4]),
    ]
    for load in loads:
        load.start()

    barrier = pltpu.get_barrier_semaphore()
    for there, where in neighbours:
        @pl.when(there)
        def _(where=where):
            pl.semaphore_signal(barrier, inc=1, device_id=where, device_id_type=MESH)
    count = sum(there.astype(jnp.int32) for there, _ in neighbours)
    pl.semaphore_wait(barrier, count)

    def remote(src, dst, send, recv, where):
        return pltpu.make_async_remote_copy(
            src_ref=src, dst_ref=dst, send_sem=send, recv_sem=recv,
            device_id=where, device_id_type=MESH,
        )

    def z_copies(side):
        edge = first if side == 0 else last
        halo = bottom if side == 0 else top
        where = {"space": s - 1} if side == 0 else {"space": s + 1}
        pairs = [
            (inc.at[:, edge], incx.at[pl.ds(1, 2), halo]),
            (crow.at[edge], cx.at[0, halo]),
            (ccol.at[edge], cx.at[1, halo]),
            (codes, codex.at[2 if side == 0 else 0]),
            (prec.at[:, edge], precx.at[:, halo]),
        ]
        return [
            remote(src, dst, zsend.at[side, i], zrecv.at[side, i], where)
            for i, (src, dst) in enumerate(pairs)
        ]

    forward = remote(inc.at[1], incx.at[0, own], tsend.at[0], trecv.at[0], {"tm": t + 1})
    relay_top = remote(incx.at[2, top], incx.at[0, top], tsend.at[1], trecv.at[1], {"tm": t + 1})
    relay_bottom = remote(incx.at[2, bottom], incx.at[0, bottom], tsend.at[2], trecv.at[2], {"tm": t + 1})

    def back_copy(i):
        part = pl.ds((parts[i][0] - 1) * BX, parts[i][1] * BX)
        return remote(img.at[part], back.at[part], bsend.at[i], brecv.at[i], {"tm": t - 1})

    @pl.when(has_next)
    def _():
        forward.start()

    sent_to = ((0, has_lo), (1, has_hi))
    arrives = ((0, has_hi), (1, has_lo))
    to_side = {0: z_copies(0), 1: z_copies(1)}
    for i in range(5):
        for side, there in sent_to:
            @pl.when(there)
            def _(side=side, i=i):
                to_side[side][i].start()

    def clear(ref_rows):
        for k in range(3):
            incx[k, ref_rows, :] = jnp.zeros((BX, cols), jnp.float32)
        for k in range(2):
            precx[k, ref_rows, :] = jnp.zeros((BX, cols), jnp.float32)
            cx[k, ref_rows, :] = jnp.zeros((BX, cols), jnp.float32)

    @pl.when(jnp.logical_not(has_lo))
    def _():
        clear(top)
        codex[0] = jnp.zeros(codex.shape[1:], jnp.int32)

    @pl.when(jnp.logical_not(has_hi))
    def _():
        clear(bottom)
        codex[2] = jnp.zeros(codex.shape[1:], jnp.int32)

    @pl.when(jnp.logical_not(has_prev))
    def _():
        incx[0] = jnp.zeros((ext, cols), jnp.float32)

    @pl.when(jnp.logical_not(has_next))
    def _():
        back[...] = jnp.zeros((rows, cols), jnp.float32)

    def arrived(i):
        for side, there in arrives:
            @pl.when(there)
            def _(side=side):
                to_side[side][i].wait_recv()

    def expand(part):
        for k in range(2):
            value = codex[part, k]
            for j in range(cols // BY):
                cexp[k, pl.ds(part * blocks, blocks), pl.ds(j * BY, BY)] = jnp.broadcast_to(
                    value[:, j : j + 1], (blocks, BY)
                )

    row = lax.broadcasted_iota(jnp.int32, (BX, cols), 0)
    is_first, is_last = row == 0, row == BX - 1

    def at(b):
        return pl.ds(pl.multiple_of(b * BX, BX), BX)

    def left(cur):
        return pltpu.roll(cur, 1, 1)

    def right(cur):
        return pltpu.roll(cur, cols - 1, 1)

    def code_of(k, b):
        return jnp.broadcast_to(cexp[k, pl.ds(b + blocks - 1, 1), :], (BX, cols))

    def stages(k, edges):
        low, high = (0, blocks + 1) if edges else (1, blocks)

        def each(body):
            def step(i, carry):
                body(i + jnp.where(i >= 2, blocks - 2, 0) if edges else i + 1)
                return carry

            trips = 4 if edges else blocks
            lax.fori_loop(0, trips, step, 0, unroll=trips)

        def above(ref, b, cur):
            prev = ref[k, at(jnp.maximum(b - 1, low)), :]
            return pltpu.roll(jnp.where(is_last, prev, cur), 1, 0)

        def below(ref, b, cur):
            after = ref[k, at(jnp.minimum(b + 1, high)), :]
            return pltpu.roll(jnp.where(is_first, after, cur), BX - 1, 0)

        def inside(b, value):
            if not edges:
                return value
            keep = ((b > 0) | has_lo) & ((b < blocks + 1) | has_hi)
            return jnp.where(keep, value, 0.0)

        def star(ref, b):
            cur = ref[k, at(b), :]
            return cur + above(ref, b, cur) + below(ref, b, cur) + (left(cur) + right(cur))

        def misfit(b):
            cur = incx[k, at(b), :]
            code = code_of(k, b)
            from_rows = jnp.where((code & 1) == 0, above(incx, b, cur), below(incx, b, cur))
            from_cols = jnp.where(code < 2, left(cur), right(cur))
            moved = cur + cx[0, at(b), :] * (from_rows - cur) + cx[1, at(b), :] * (from_cols - cur)
            ms[k, at(b), :] = inside(b, incx[k + 1, at(b), :] - moved)

        def first_sweep(b):
            f1[k, at(b), :] = inside(b, star(ms, b))

        def second_sweep(b):
            f2[k, at(b), :] = inside(b, precx[k, at(b), :] * star(f1, b))

        def third_sweep(b):
            f3[k, at(b), :] = inside(b, star(f2, b))

        def weigh(b):
            value = inside(b, star(f3, b) * (0.2 ** (2 * SWEEPS)))
            lower = (code_of(k, b) & 1) == 0
            along = cx[0, at(b), :] * value
            w[k, at(b), :] = value
            dn[k, at(b), :] = jnp.where(lower, along, 0.0)
            up_[k, at(b), :] = jnp.where(lower, 0.0, along)

        for body in (misfit, first_sweep, second_sweep, third_sweep, weigh):
            each(body)

    def retreat(k, start, size):
        def body(i, carry):
            b = i + start
            value = w[k, at(b), :]
            d, u = dn[k, at(b), :], up_[k, at(b), :]
            after, prev = dn[k, at(b + 1), :], up_[k, at(b - 1), :]
            along = cx[1, at(b), :] * value
            plus = jnp.where(code_of(k, b) < 2, along, 0.0)
            image = (
                value - (d + u) - along
                + pltpu.roll(jnp.where(is_first, after, d), BX - 1, 0)
                + pltpu.roll(jnp.where(is_last, prev, u), 1, 0)
                + right(plus) + left(along - plus)
            )
            if k == 0:
                img[at(b - 1), :] = image
            else:
                adj[0, at(b - 1), :] = w[0, at(b), :] - image
            return carry

        lax.fori_loop(0, size, body, 0, unroll=size)

    def send_back(i):
        retreat(0, *parts[i])

        @pl.when(has_prev)
        def _():
            back_copy(i).start()

    for i in (0, 1, 2, 3):
        loads[i].wait()
    expand(1)
    loads[4].wait()
    stages(1, False)

    arrived(0)

    @pl.when(has_next & has_lo)
    def _():
        relay_top.start()

    @pl.when(has_next & has_hi)
    def _():
        relay_bottom.start()

    @pl.when(has_prev)
    def _():
        forward.wait_recv()

    stages(0, False)
    for i in range(len(parts) - 2):
        send_back(i)

    for i in (1, 2, 3, 4):
        arrived(i)
    expand(0)
    expand(2)

    @pl.when(has_prev & has_lo)
    def _():
        relay_top.wait_recv()

    @pl.when(has_prev & has_hi)
    def _():
        relay_bottom.wait_recv()

    stages(0, True)
    for i in (len(parts) - 2, len(parts) - 1):
        send_back(i)
    stages(1, True)
    misfit_copies = [
        pltpu.make_async_copy(ms.at[k, own], misfit_out.at[k], out_sem.at[k]) for k in range(2)
    ]
    for copy in misfit_copies:
        copy.start()
    retreat(1, 1, blocks)

    for i, (start, size) in enumerate(parts):
        @pl.when(has_next)
        def _(i=i):
            back_copy(i).wait_recv()

        for b in range(start, start + size):
            adj[1, at(b - 1), :] = w[1, at(b), :] - back[at(b - 1), :]

    for side, there in sent_to:
        @pl.when(there)
        def _(side=side):
            for copy in to_side[side]:
                copy.wait_send()

    @pl.when(has_next)
    def _():
        forward.wait_send()

    @pl.when(has_next & has_lo)
    def _():
        relay_top.wait_send()

    @pl.when(has_next & has_hi)
    def _():
        relay_bottom.wait_send()

    @pl.when(has_prev)
    def _():
        for i in range(len(parts)):
            back_copy(i).wait_send()

    for copy in misfit_copies:
        copy.wait()


def on_device(increments, precision, courant_rows, courant_cols, wind_codes):
    steps, rows, cols = increments.shape
    ext = rows + 2 * BX
    f32 = jnp.float32
    in_vmem = pl.BlockSpec(memory_space=pltpu.MemorySpace.VMEM)
    in_hbm = pl.BlockSpec(memory_space=pltpu.MemorySpace.HBM)
    out = jax.ShapeDtypeStruct(increments.shape, f32)
    field = pltpu.VMEM((2, ext, cols), f32)
    dma = pltpu.SemaphoreType.DMA
    return pl.pallas_call(
        kernel,
        name="window",
        out_shape=(out, out),
        in_specs=[in_hbm] * 5,
        out_specs=(in_vmem, in_vmem),
        scratch_shapes=[
            pltpu.VMEM((3, ext, cols), f32),
            field,
            field,
            pltpu.VMEM((3,) + wind_codes.shape, jnp.int32),
            pltpu.VMEM((2, 3 * (rows // BX), cols), jnp.int32),
            field,
            field,
            field,
            field,
            field,
            field,
            field,
            pltpu.VMEM((rows, cols), f32),
            pltpu.VMEM((rows, cols), f32),
            dma((5,)),
            dma((2,)),
            dma((2, 5)),
            dma((2, 5)),
            dma((3,)),
            dma((3,)),
            dma((len(chunks_of(rows // BX)),)),
            dma((len(chunks_of(rows // BX)),)),
        ],
        compiler_params=pltpu.CompilerParams(
            collective_id=0, has_side_effects=True, vmem_limit_bytes=24 << 20
        ),
    )(*(pltpu.with_memory_space_constraint(x, pltpu.MemorySpace.HBM) for x in (increments, precision, courant_rows, courant_cols, wind_codes)))


def solution(mesh):
    in_specs = (
        P("tm", "space", None),
        P("tm", "space", None),
        P("space", None),
        P("space", None),
        P("tm", "space", None),
    )
    out_specs = (P("tm", "space", None), P("tm", "space", None))
    return jax.shard_map(
        on_device, mesh=mesh, in_specs=in_specs, out_specs=out_specs, check_vma=False
    )
```

```python
import functools

import jax
import jax.numpy as jnp
from jax import lax
from jax.experimental import pallas as pl
from jax.experimental.pallas import tpu as pltpu
from jax.sharding import PartitionSpec as P

BX = 8
BY = 128
SWEEPS = 2
MESH = pl.DeviceIdType.MESH


def chunks_of(blocks):
    half = blocks // 2
    middle = [(2, half - 2), (half, (blocks - half) // 2)]
    middle.append((sum(middle[1]), blocks - sum(middle[1])))
    return middle + [(1, 1), (blocks, 1)]


def kernel(
    inc, prec, crow, ccol, codes,
    misfit_out, adj,
    incx, precx, cx, codex, cexp, ms, f1, f2, f3, w, dn, up_, img, back,
    local_sem, out_sem, zsend, zrecv, tsend, trecv, bsend, brecv,
):
    rows, cols = crow.shape
    blocks = rows // BX
    ext = rows + 2 * BX
    s = lax.axis_index("space")
    t = lax.axis_index("tm")
    n_s = lax.axis_size("space")
    n_t = lax.axis_size("tm")
    has_lo, has_hi = s > 0, s < n_s - 1
    has_prev, has_next = t > 0, t < n_t - 1
    own = pl.ds(BX, rows)
    top = pl.ds(0, BX)
    bottom = pl.ds(BX + rows, BX)
    first = pl.ds(0, BX)
    last = pl.ds(rows - BX, BX)
    parts = chunks_of(blocks)

    neighbours = (
        (has_lo, {"space": s - 1}),
        (has_hi, {"space": s + 1}),
        (has_prev, {"tm": t - 1}),
        (has_next, {"tm": t + 1}),
    )

    loads = [
        pltpu.make_async_copy(inc, incx.at[pl.ds(1, 2), own], local_sem.at[0]),
        pltpu.make_async_copy(crow, cx.at[0, own], local_sem.at[1]),
        pltpu.make_async_copy(ccol, cx.at[1, own], local_sem.at[2]),
        pltpu.make_async_copy(codes, codex.at[1], local_sem.at[3]),
        pltpu.make_async_copy(prec, precx.at[:, own], local_sem.at[4]),
    ]
    for load in loads:
        load.start()

    barrier = pltpu.get_barrier_semaphore()
    for there, where in neighbours:
        @pl.when(there)
        def _(where=where):
            pl.semaphore_signal(barrier, inc=1, device_id=where, device_id_type=MESH)
    count = sum(there.astype(jnp.int32) for there, _ in neighbours)
    pl.semaphore_wait(barrier, count)

    def remote(src, dst, send, recv, where):
        return pltpu.make_async_remote_copy(
            src_ref=src, dst_ref=dst, send_sem=send, recv_sem=recv,
            device_id=where, device_id_type=MESH,
        )

    def z_copies(side):
        edge = first if side == 0 else last
        halo = bottom if side == 0 else top
        where = {"space": s - 1} if side == 0 else {"space": s + 1}
        pairs = [
            (inc.at[:, edge], incx.at[pl.ds(1, 2), halo]),
            (crow.at[edge], cx.at[0, halo]),
            (ccol.at[edge], cx.at[1, halo]),
            (codes, codex.at[2 if side == 0 else 0]),
            (prec.at[:, edge], precx.at[:, halo]),
        ]
        return [
            remote(src, dst, zsend.at[side, i], zrecv.at[side, i], where)
            for i, (src, dst) in enumerate(pairs)
        ]

    half = blocks // 2
    forward = [
        remote(
            inc.at[1, pl.ds(start * BX, size * BX)],
            incx.at[0, pl.ds((start + 1) * BX, size * BX)],
            tsend.at[sem], trecv.at[sem], {"tm": t + 1},
        )
        for sem, start, size in ((0, 0, half), (3, half, blocks - half))
    ]
    relay_top = remote(incx.at[2, top], incx.at[0, top], tsend.at[1], trecv.at[1], {"tm": t + 1})
    relay_bottom = remote(incx.at[2, bottom], incx.at[0, bottom], tsend.at[2], trecv.at[2], {"tm": t + 1})

    def back_copy(i):
        part = pl.ds((parts[i][0] - 1) * BX, parts[i][1] * BX)
        return remote(img.at[part], back.at[part], bsend.at[i], brecv.at[i], {"tm": t - 1})

    @pl.when(has_next)
    def _():
        for copy in forward:
            copy.start()

    sent_to = ((0, has_lo), (1, has_hi))
    arrives = ((0, has_hi), (1, has_lo))
    to_side = {0: z_copies(0), 1: z_copies(1)}
    for i in range(5):
        for side, there in sent_to:
            @pl.when(there)
            def _(side=side, i=i):
                to_side[side][i].start()

    def clear(ref_rows):
        for k in range(3):
            incx[k, ref_rows, :] = jnp.zeros((BX, cols), jnp.float32)
        for k in range(2):
            precx[k, ref_rows, :] = jnp.zeros((BX, cols), jnp.float32)
            cx[k, ref_rows, :] = jnp.zeros((BX, cols), jnp.float32)

    @pl.when(jnp.logical_not(has_lo))
    def _():
        clear(top)
        codex[0] = jnp.zeros(codex.shape[1:], jnp.int32)

    @pl.when(jnp.logical_not(has_hi))
    def _():
        clear(bottom)
        codex[2] = jnp.zeros(codex.shape[1:], jnp.int32)

    @pl.when(jnp.logical_not(has_prev))
    def _():
        incx[0] = jnp.zeros((ext, cols), jnp.float32)

    @pl.when(jnp.logical_not(has_next))
    def _():
        back[...] = jnp.zeros((rows, cols), jnp.float32)

    def arrived(i):
        for side, there in arrives:
            @pl.when(there)
            def _(side=side):
                to_side[side][i].wait_recv()

    def expand(part):
        for k in range(2):
            value = codex[part, k]
            for j in range(cols // BY):
                cexp[k, pl.ds(part * blocks, blocks), pl.ds(j * BY, BY)] = jnp.broadcast_to(
                    value[:, j : j + 1], (blocks, BY)
                )

    row = lax.broadcasted_iota(jnp.int32, (BX, cols), 0)
    is_first, is_last = row == 0, row == BX - 1

    def at(b):
        return pl.ds(pl.multiple_of(b * BX, BX), BX)

    def left(cur):
        return pltpu.roll(cur, 1, 1)

    def right(cur):
        return pltpu.roll(cur, cols - 1, 1)

    def code_of(k, b):
        return jnp.broadcast_to(cexp[k, pl.ds(b + blocks - 1, 1), :], (BX, cols))

    def stages(k, begin, end, low, high, edges=False):

        def each(body):
            def step(i, carry):
                body(i + jnp.where(i >= 2, blocks - 2, 0) if edges else i + begin)
                return carry

            trips = 4 if edges else end - begin + 1
            lax.fori_loop(0, trips, step, 0, unroll=trips)

        def above(ref, b, cur):
            prev = ref[k, at(jnp.maximum(b - 1, low)), :]
            return pltpu.roll(jnp.where(is_last, prev, cur), 1, 0)

        def below(ref, b, cur):
            after = ref[k, at(jnp.minimum(b + 1, high)), :]
            return pltpu.roll(jnp.where(is_first, after, cur), BX - 1, 0)

        def inside(b, value):
            if not edges:
                return value
            keep = ((b > 0) | has_lo) & ((b < blocks + 1) | has_hi)
            return jnp.where(keep, value, 0.0)

        def star(ref, b):
            cur = ref[k, at(b), :]
            return cur + above(ref, b, cur) + below(ref, b, cur) + (left(cur) + right(cur))

        def misfit(b):
            cur = incx[k, at(b), :]
            code = code_of(k, b)
            from_rows = jnp.where((code & 1) == 0, above(incx, b, cur), below(incx, b, cur))
            from_cols = jnp.where(code < 2, left(cur), right(cur))
            moved = cur + cx[0, at(b), :] * (from_rows - cur) + cx[1, at(b), :] * (from_cols - cur)
            ms[k, at(b), :] = inside(b, incx[k + 1, at(b), :] - moved)

        def first_sweep(b):
            f1[k, at(b), :] = inside(b, star(ms, b))

        def second_sweep(b):
            f2[k, at(b), :] = inside(b, precx[k, at(b), :] * star(f1, b))

        def third_sweep(b):
            f3[k, at(b), :] = inside(b, star(f2, b))

        def weigh(b):
            value = inside(b, star(f3, b) * (0.2 ** (2 * SWEEPS)))
            lower = (code_of(k, b) & 1) == 0
            along = cx[0, at(b), :] * value
            w[k, at(b), :] = value
            dn[k, at(b), :] = jnp.where(lower, along, 0.0)
            up_[k, at(b), :] = jnp.where(lower, 0.0, along)

        for body in (misfit, first_sweep, second_sweep, third_sweep, weigh):
            each(body)

    def retreat(k, start, size):
        def body(i, carry):
            b = i + start
            value = w[k, at(b), :]
            d, u = dn[k, at(b), :], up_[k, at(b), :]
            after, prev = dn[k, at(b + 1), :], up_[k, at(b - 1), :]
            along = cx[1, at(b), :] * value
            plus = jnp.where(code_of(k, b) < 2, along, 0.0)
            image = (
                value - (d + u) - along
                + pltpu.roll(jnp.where(is_first, after, d), BX - 1, 0)
                + pltpu.roll(jnp.where(is_last, prev, u), 1, 0)
                + right(plus) + left(along - plus)
            )
            if k == 0:
                img[at(b - 1), :] = image
            else:
                adj[0, at(b - 1), :] = w[0, at(b), :] - image
            return carry

        lax.fori_loop(0, size, body, 0, unroll=size)

    def send_back(i):
        retreat(0, *parts[i])

        @pl.when(has_prev)
        def _():
            back_copy(i).start()

    for i in (0, 1, 2, 3):
        loads[i].wait()
    expand(1)
    loads[4].wait()
    stages(1, 1, blocks, 1, blocks)

    arrived(0)

    @pl.when(has_next & has_lo)
    def _():
        relay_top.start()

    @pl.when(has_next & has_hi)
    def _():
        relay_bottom.start()

    @pl.when(has_prev)
    def _():
        forward[0].wait_recv()

    stages(0, 1, half, 1, half)
    send_back(0)

    @pl.when(has_prev)
    def _():
        forward[1].wait_recv()

    stages(0, half, blocks, half - 1, blocks)
    for i in range(1, len(parts) - 2):
        send_back(i)

    for i in (1, 2, 3, 4):
        arrived(i)
    expand(0)
    expand(2)

    @pl.when(has_prev & has_lo)
    def _():
        relay_top.wait_recv()

    @pl.when(has_prev & has_hi)
    def _():
        relay_bottom.wait_recv()

    stages(0, 0, blocks + 1, 0, blocks + 1, edges=True)
    for i in (len(parts) - 2, len(parts) - 1):
        send_back(i)
    stages(1, 0, blocks + 1, 0, blocks + 1, edges=True)
    misfit_copies = [
        pltpu.make_async_copy(ms.at[k, own], misfit_out.at[k], out_sem.at[k]) for k in range(2)
    ]
    for copy in misfit_copies:
        copy.start()
    retreat(1, 1, blocks)

    for i, (start, size) in enumerate(parts):
        @pl.when(has_next)
        def _(i=i):
            back_copy(i).wait_recv()

        for b in range(start, start + size):
            adj[1, at(b - 1), :] = w[1, at(b), :] - back[at(b - 1), :]

    for side, there in sent_to:
        @pl.when(there)
        def _(side=side):
            for copy in to_side[side]:
                copy.wait_send()

    @pl.when(has_next)
    def _():
        for copy in forward:
            copy.wait_send()

    @pl.when(has_next & has_lo)
    def _():
        relay_top.wait_send()

    @pl.when(has_next & has_hi)
    def _():
        relay_bottom.wait_send()

    @pl.when(has_prev)
    def _():
        for i in range(len(parts)):
            back_copy(i).wait_send()

    for copy in misfit_copies:
        copy.wait()


def on_device(increments, precision, courant_rows, courant_cols, wind_codes):
    steps, rows, cols = increments.shape
    ext = rows + 2 * BX
    f32 = jnp.float32
    in_vmem = pl.BlockSpec(memory_space=pltpu.MemorySpace.VMEM)
    in_hbm = pl.BlockSpec(memory_space=pltpu.MemorySpace.HBM)
    out = jax.ShapeDtypeStruct(increments.shape, f32)
    field = pltpu.VMEM((2, ext, cols), f32)
    dma = pltpu.SemaphoreType.DMA
    return pl.pallas_call(
        kernel,
        name="window",
        out_shape=(out, out),
        in_specs=[in_hbm] * 5,
        out_specs=(in_vmem, in_vmem),
        scratch_shapes=[
            pltpu.VMEM((3, ext, cols), f32),
            field,
            field,
            pltpu.VMEM((3,) + wind_codes.shape, jnp.int32),
            pltpu.VMEM((2, 3 * (rows // BX), cols), jnp.int32),
            field,
            field,
            field,
            field,
            field,
            field,
            field,
            pltpu.VMEM((rows, cols), f32),
            pltpu.VMEM((rows, cols), f32),
            dma((5,)),
            dma((2,)),
            dma((2, 5)),
            dma((2, 5)),
            dma((4,)),
            dma((4,)),
            dma((len(chunks_of(rows // BX)),)),
            dma((len(chunks_of(rows // BX)),)),
        ],
        compiler_params=pltpu.CompilerParams(
            collective_id=0, has_side_effects=True, vmem_limit_bytes=24 << 20
        ),
    )(*(pltpu.with_memory_space_constraint(x, pltpu.MemorySpace.HBM) for x in (increments, precision, courant_rows, courant_cols, wind_codes)))


def solution(mesh):
    in_specs = (
        P("tm", "space", None),
        P("tm", "space", None),
        P("space", None),
        P("space", None),
        P("tm", "space", None),
    )
    out_specs = (P("tm", "space", None), P("tm", "space", None))
    return jax.shard_map(
        on_device, mesh=mesh, in_specs=in_specs, out_specs=out_specs, check_vma=False
    )
```

```python
import functools

import jax
import jax.numpy as jnp
from jax import lax
from jax.experimental import pallas as pl
from jax.experimental.pallas import tpu as pltpu
from jax.sharding import PartitionSpec as P

BX = 8
BY = 128
SWEEPS = 2
MESH = pl.DeviceIdType.MESH


def chunks_of(blocks):
    half = blocks // 2
    middle = [(2, half - 2), (half, (blocks - half) // 2)]
    middle.append((sum(middle[1]), blocks - sum(middle[1])))
    return middle + [(1, 1), (blocks, 1)]


def kernel(
    inc, prec, crow, ccol, codes,
    misfit_out, adj,
    incx, precx, cx, codex, cexp, ms, f1, f2, f3, w, dn, up_, img, back,
    local_sem, out_sem, zsend, zrecv, tsend, trecv, bsend, brecv,
):
    rows, cols = crow.shape
    blocks = rows // BX
    ext = rows + 2 * BX
    s = lax.axis_index("space")
    t = lax.axis_index("tm")
    n_s = lax.axis_size("space")
    n_t = lax.axis_size("tm")
    has_lo, has_hi = s > 0, s < n_s - 1
    has_prev, has_next = t > 0, t < n_t - 1
    own = pl.ds(BX, rows)
    top = pl.ds(0, BX)
    bottom = pl.ds(BX + rows, BX)
    depths = (2 * SWEEPS + 2, 2 * SWEEPS + 1, SWEEPS + 1)
    parts = chunks_of(blocks)

    neighbours = (
        (has_lo, {"space": s - 1}),
        (has_hi, {"space": s + 1}),
        (has_prev, {"tm": t - 1}),
        (has_next, {"tm": t + 1}),
    )

    loads = [
        pltpu.make_async_copy(inc, incx.at[pl.ds(1, 2), own], local_sem.at[0]),
        pltpu.make_async_copy(crow, cx.at[0, own], local_sem.at[1]),
        pltpu.make_async_copy(ccol, cx.at[1, own], local_sem.at[2]),
        pltpu.make_async_copy(codes, codex.at[1], local_sem.at[3]),
        pltpu.make_async_copy(prec, precx.at[:, own], local_sem.at[4]),
    ]
    for load in loads:
        load.start()

    barrier = pltpu.get_barrier_semaphore()
    for there, where in neighbours:
        @pl.when(there)
        def _(where=where):
            pl.semaphore_signal(barrier, inc=1, device_id=where, device_id_type=MESH)
    count = sum(there.astype(jnp.int32) for there, _ in neighbours)
    pl.semaphore_wait(barrier, count)

    def remote(src, dst, send, recv, where):
        return pltpu.make_async_remote_copy(
            src_ref=src, dst_ref=dst, send_sem=send, recv_sem=recv,
            device_id=where, device_id_type=MESH,
        )

    def halo_rows(side, n):
        return pl.ds(BX + rows if side == 0 else BX - n, n)

    def z_copies(side):
        where = {"space": s - 1} if side == 0 else {"space": s + 1}
        edge = [pl.ds(0 if side == 0 else rows - n, n) for n in depths]
        halo = [halo_rows(side, n) for n in depths]
        pairs = [
            (inc.at[:, edge[0]], incx.at[pl.ds(1, 2), halo[0]]),
            (crow.at[edge[1]], cx.at[0, halo[1]]),
            (ccol.at[edge[1]], cx.at[1, halo[1]]),
            (codes, codex.at[2 if side == 0 else 0]),
            (prec.at[:, edge[2]], precx.at[:, halo[2]]),
        ]
        return [
            remote(src, dst, zsend.at[side, i], zrecv.at[side, i], where)
            for i, (src, dst) in enumerate(pairs)
        ]

    half = blocks // 2
    forward = [
        remote(
            inc.at[1, pl.ds(start * BX, size * BX)],
            incx.at[0, pl.ds((start + 1) * BX, size * BX)],
            tsend.at[sem], trecv.at[sem], {"tm": t + 1},
        )
        for sem, start, size in ((0, 0, half), (3, half, blocks - half))
    ]
    relay_top = remote(
        incx.at[2, halo_rows(1, depths[0])], incx.at[0, halo_rows(1, depths[0])], tsend.at[1], trecv.at[1], {"tm": t + 1})
    relay_bottom = remote(
        incx.at[2, halo_rows(0, depths[0])], incx.at[0, halo_rows(0, depths[0])], tsend.at[2], trecv.at[2], {"tm": t + 1})

    def back_copy(i):
        part = pl.ds((parts[i][0] - 1) * BX, parts[i][1] * BX)
        return remote(img.at[part], back.at[part], bsend.at[i], brecv.at[i], {"tm": t - 1})

    @pl.when(has_next)
    def _():
        for copy in forward:
            copy.start()

    sent_to = ((0, has_lo), (1, has_hi))
    arrives = ((0, has_hi), (1, has_lo))
    to_side = {0: z_copies(0), 1: z_copies(1)}
    for i in range(5):
        for side, there in sent_to:
            @pl.when(there)
            def _(side=side, i=i):
                to_side[side][i].start()

    def clear(ref_rows):
        for k in range(3):
            incx[k, ref_rows, :] = jnp.zeros((BX, cols), jnp.float32)
        for k in range(2):
            precx[k, ref_rows, :] = jnp.zeros((BX, cols), jnp.float32)
            cx[k, ref_rows, :] = jnp.zeros((BX, cols), jnp.float32)

    @pl.when(jnp.logical_not(has_lo))
    def _():
        clear(top)
        codex[0] = jnp.zeros(codex.shape[1:], jnp.int32)

    @pl.when(jnp.logical_not(has_hi))
    def _():
        clear(bottom)
        codex[2] = jnp.zeros(codex.shape[1:], jnp.int32)

    @pl.when(jnp.logical_not(has_prev))
    def _():
        incx[0] = jnp.zeros((ext, cols), jnp.float32)

    @pl.when(jnp.logical_not(has_next))
    def _():
        back[...] = jnp.zeros((rows, cols), jnp.float32)

    def arrived(i):
        for side, there in arrives:
            @pl.when(there)
            def _(side=side):
                to_side[side][i].wait_recv()

    def expand(part):
        for k in range(2):
            value = codex[part, k]
            for j in range(cols // BY):
                cexp[k, pl.ds(part * blocks, blocks), pl.ds(j * BY, BY)] = jnp.broadcast_to(
                    value[:, j : j + 1], (blocks, BY)
                )

    row = lax.broadcasted_iota(jnp.int32, (BX, cols), 0)
    is_first, is_last = row == 0, row == BX - 1

    def at(b):
        return pl.ds(pl.multiple_of(b * BX, BX), BX)

    def left(cur):
        return pltpu.roll(cur, 1, 1)

    def right(cur):
        return pltpu.roll(cur, cols - 1, 1)

    def code_of(k, b):
        return jnp.broadcast_to(cexp[k, pl.ds(b + blocks - 1, 1), :], (BX, cols))

    def stages(k, begin, end, low, high, edges=False):

        def each(body):
            def step(i, carry):
                body(i + jnp.where(i >= 2, blocks - 2, 0) if edges else i + begin)
                return carry

            trips = 4 if edges else end - begin + 1
            lax.fori_loop(0, trips, step, 0, unroll=trips)

        def above(ref, b, cur):
            prev = ref[k, at(jnp.maximum(b - 1, low)), :]
            return pltpu.roll(jnp.where(is_last, prev, cur), 1, 0)

        def below(ref, b, cur):
            after = ref[k, at(jnp.minimum(b + 1, high)), :]
            return pltpu.roll(jnp.where(is_first, after, cur), BX - 1, 0)

        def inside(b, value):
            if not edges:
                return value
            keep = ((b > 0) | has_lo) & ((b < blocks + 1) | has_hi)
            return jnp.where(keep, value, 0.0)

        def star(ref, b):
            cur = ref[k, at(b), :]
            return cur + above(ref, b, cur) + below(ref, b, cur) + (left(cur) + right(cur))

        def misfit(b):
            cur = incx[k, at(b), :]
            code = code_of(k, b)
            from_rows = jnp.where((code & 1) == 0, above(incx, b, cur), below(incx, b, cur))
            from_cols = jnp.where(code < 2, left(cur), right(cur))
            moved = cur + cx[0, at(b), :] * (from_rows - cur) + cx[1, at(b), :] * (from_cols - cur)
            ms[k, at(b), :] = inside(b, incx[k + 1, at(b), :] - moved)

        def first_sweep(b):
            f1[k, at(b), :] = inside(b, star(ms, b))

        def second_sweep(b):
            f2[k, at(b), :] = inside(b, precx[k, at(b), :] * star(f1, b))

        def third_sweep(b):
            f3[k, at(b), :] = inside(b, star(f2, b))

        def weigh(b):
            value = inside(b, star(f3, b) * (0.2 ** (2 * SWEEPS)))
            lower = (code_of(k, b) & 1) == 0
            along = cx[0, at(b), :] * value
            w[k, at(b), :] = value
            dn[k, at(b), :] = jnp.where(lower, along, 0.0)
            up_[k, at(b), :] = jnp.where(lower, 0.0, along)

        for body in (misfit, first_sweep, second_sweep, third_sweep, weigh):
            each(body)

    def retreat(k, start, size):
        def body(i, carry):
            b = i + start
            value = w[k, at(b), :]
            d, u = dn[k, at(b), :], up_[k, at(b), :]
            after, prev = dn[k, at(b + 1), :], up_[k, at(b - 1), :]
            along = cx[1, at(b), :] * value
            plus = jnp.where(code_of(k, b) < 2, along, 0.0)
            image = (
                value - (d + u) - along
                + pltpu.roll(jnp.where(is_first, after, d), BX - 1, 0)
                + pltpu.roll(jnp.where(is_last, prev, u), 1, 0)
                + right(plus) + left(along - plus)
            )
            if k == 0:
                img[at(b - 1), :] = image
            else:
                adj[0, at(b - 1), :] = w[0, at(b), :] - image
            return carry

        lax.fori_loop(0, size, body, 0, unroll=size)

    def send_back(i):
        retreat(0, *parts[i])

        @pl.when(has_prev)
        def _():
            back_copy(i).start()

    for i in (0, 1, 2, 3):
        loads[i].wait()
    expand(1)
    loads[4].wait()
    stages(1, 1, blocks, 1, blocks)

    arrived(0)

    @pl.when(has_next & has_lo)
    def _():
        relay_top.start()

    @pl.when(has_next & has_hi)
    def _():
        relay_bottom.start()

    @pl.when(has_prev)
    def _():
        forward[0].wait_recv()

    stages(0, 1, half, 1, half)
    send_back(0)

    @pl.when(has_prev)
    def _():
        forward[1].wait_recv()

    stages(0, half, blocks, half - 1, blocks)
    for i in range(1, len(parts) - 2):
        send_back(i)

    for i in (1, 2, 3, 4):
        arrived(i)
    expand(0)
    expand(2)

    @pl.when(has_prev & has_lo)
    def _():
        relay_top.wait_recv()

    @pl.when(has_prev & has_hi)
    def _():
        relay_bottom.wait_recv()

    stages(0, 0, blocks + 1, 0, blocks + 1, edges=True)
    for i in (len(parts) - 2, len(parts) - 1):
        send_back(i)
    stages(1, 0, blocks + 1, 0, blocks + 1, edges=True)
    misfit_copies = [
        pltpu.make_async_copy(ms.at[k, own], misfit_out.at[k], out_sem.at[k]) for k in range(2)
    ]
    for copy in misfit_copies:
        copy.start()
    retreat(1, 1, blocks)

    for i, (start, size) in enumerate(parts):
        @pl.when(has_next)
        def _(i=i):
            back_copy(i).wait_recv()

        for b in range(start, start + size):
            adj[1, at(b - 1), :] = w[1, at(b), :] - back[at(b - 1), :]

    for side, there in sent_to:
        @pl.when(there)
        def _(side=side):
            for copy in to_side[side]:
                copy.wait_send()

    @pl.when(has_next)
    def _():
        for copy in forward:
            copy.wait_send()

    @pl.when(has_next & has_lo)
    def _():
        relay_top.wait_send()

    @pl.when(has_next & has_hi)
    def _():
        relay_bottom.wait_send()

    @pl.when(has_prev)
    def _():
        for i in range(len(parts)):
            back_copy(i).wait_send()

    for copy in misfit_copies:
        copy.wait()


def on_device(increments, precision, courant_rows, courant_cols, wind_codes):
    steps, rows, cols = increments.shape
    ext = rows + 2 * BX
    f32 = jnp.float32
    in_vmem = pl.BlockSpec(memory_space=pltpu.MemorySpace.VMEM)
    in_hbm = pl.BlockSpec(memory_space=pltpu.MemorySpace.HBM)
    out = jax.ShapeDtypeStruct(increments.shape, f32)
    field = pltpu.VMEM((2, ext, cols), f32)
    dma = pltpu.SemaphoreType.DMA
    return pl.pallas_call(
        kernel,
        name="window",
        out_shape=(out, out),
        in_specs=[in_hbm] * 5,
        out_specs=(in_vmem, in_vmem),
        scratch_shapes=[
            pltpu.VMEM((3, ext, cols), f32),
            field,
            field,
            pltpu.VMEM((3,) + wind_codes.shape, jnp.int32),
            pltpu.VMEM((2, 3 * (rows // BX), cols), jnp.int32),
            field,
            field,
            field,
            field,
            field,
            field,
            field,
            pltpu.VMEM((rows, cols), f32),
            pltpu.VMEM((rows, cols), f32),
            dma((5,)),
            dma((2,)),
            dma((2, 5)),
            dma((2, 5)),
            dma((4,)),
            dma((4,)),
            dma((len(chunks_of(rows // BX)),)),
            dma((len(chunks_of(rows // BX)),)),
        ],
        compiler_params=pltpu.CompilerParams(
            collective_id=0, has_side_effects=True, vmem_limit_bytes=24 << 20
        ),
    )(*(pltpu.with_memory_space_constraint(x, pltpu.MemorySpace.HBM) for x in (increments, precision, courant_rows, courant_cols, wind_codes)))


def solution(mesh):
    in_specs = (
        P("tm", "space", None),
        P("tm", "space", None),
        P("space", None),
        P("space", None),
        P("tm", "space", None),
    )
    out_specs = (P("tm", "space", None), P("tm", "space", None))
    return jax.shard_map(
        on_device, mesh=mesh, in_specs=in_specs, out_specs=out_specs, check_vma=False
    )
```
